1024 devices in a mesh: dp: 8 (over y), expert: 64 (over x, z), mp: 2 (over core).
Axes of the slice: x: 8, y: 8, z: 8, core: 2. Of those that a mesh axis runs over, the one named last changes fastest.
Arguments:
- tokens: float32 [65536, 1024], P(('dp', 'expert')), may hold values from -24 to 24
- block_experts: int32 [16384, 1], P(('dp', 'expert')), may hold values from 0 to 63, as said below
- weight_up: bfloat16 [64, 1024, 2048], P('expert', None, 'mp'), may hold values from -0.1875 to 0.1875
- weight_down: bfloat16 [64, 2048, 1024], P('expert', 'mp'), may hold values from -0.125 to 0.125
- upstream: float32 [65536, 1024], P(('dp', 'expert')), may hold values from -24 to 24
Outputs:
- layer_output: float32 [65536, 1024], P(('dp', 'expert'))
- grad_tokens: float32 [65536, 1024], P(('dp', 'expert'))
- grad_up: float32 [64, 1024, 2048], P('expert', 'dp', 'mp')
- grad_down: float32 [64, 2048, 1024], P('expert', 'mp', 'dp')
The draws below stay inside these ranges and needn't reach their ends.
Inputs may be any that keep to these rules, and one draw needn't show every extreme that they name: `block_experts`: of the 32 cell blocks of one device, at most 1 name the same expert, and in every draw some expert is named by exactly 1 block of every device.
All inputs are finite; a program needn't handle non-finite values.
Results may differ from the reference program's by a relative error of at most 0.015.
Values may be sent and summed in bfloat16 or wider, within the bound.
No kernel may reach another device: no remote copies, remote signals or barrier semaphores. Data moves between devices by JAX's collectives and lax.ppermute only.
A program may use at most 64 MiB of HBM per device.

```python
import jax
import jax.numpy as jnp
from jax import lax

D = 1024
FF = 2048
BLOCK = 4
EXPERTS = 64
BLOCKS_DEV = 32
CAP = 1
TOKENS = 65536
BLOCKS = 16384
N_DP = 8
N_EXPERT = 64


def draw_block_experts(key, part):
    device_count = BLOCKS // BLOCKS_DEV
    slot_total = EXPERTS * CAP
    hot_count = max(1, BLOCKS_DEV // (4 * CAP))
    expert_rank = jax.random.permutation(jax.random.fold_in(key, 1), EXPERTS).astype(jnp.int32)
    slot_ids = jnp.arange(slot_total, dtype=jnp.int32)
    slot_rank = expert_rank[slot_ids // CAP]
    base_score = jnp.where(slot_rank < hot_count, 1 << 20, 0).astype(jnp.int32) + (EXPERTS - slot_rank)

    def draw_device(device_key):
        noise_draw = jax.random.randint(jax.random.fold_in(device_key, 2), (slot_total,), 0, EXPERTS, dtype=jnp.int32)
        score_all = (base_score + noise_draw) * slot_total + slot_ids
        top_vals, top_idx = lax.top_k(score_all, BLOCKS_DEV)
        chosen = (top_idx // CAP).astype(jnp.int32)
        shuffle = jax.random.permutation(jax.random.fold_in(device_key, 3), BLOCKS_DEV)
        return chosen[shuffle]
    device_keys = jax.random.split(jax.random.fold_in(key, 4), device_count)
    return jax.vmap(draw_device)(device_keys).reshape(BLOCKS, 1).astype(jnp.int32)


def spiked(entries, rng, source, target, blocks, factor):
    owner, partner = [(jnp.arange(entries.shape[axis_at]) // (entries.shape[axis_at] // blocks)).reshape([-1 if axis == axis_at else 1 for axis in range(entries.ndim)]) for axis_at in (source, target)]
    chosen = jax.random.permutation(rng, blocks)[partner]
    strong = (owner == chosen) | (owner == (partner + blocks // 2) % blocks)
    return jnp.where(strong, factor * entries, entries)


def level_of(key, dims, cuts, low, top_value):
    factor_of = 1.0
    for dim, parts in cuts:
        steps = jax.random.uniform(jax.random.fold_in(jax.random.fold_in(key, 6), dim), (parts,), jnp.float32, low / len(cuts), top_value / len(cuts))
        factor_of = factor_of * jnp.repeat(jnp.exp(steps), dims[dim] // parts).reshape((-1,) + (1,) * (len(dims) - 1 - dim))
    return factor_of


def noise(rng, extent, deviation, limit, shards=(), kind=jnp.bfloat16):
    entries = deviation * jax.random.normal(rng, extent, jnp.float32)
    if shards:
        entries = entries * level_of(rng, extent, shards, -0.22, 0.18)
    return jnp.clip(entries, -limit, limit).astype(kind)


def noise_with(rng, extent, spread, limit, shards, heavy, held_as=jnp.bfloat16):
    array = spread * jax.random.normal(rng, extent, jnp.float32)
    if shards:
        array = array * level_of(rng, extent, shards, -0.22, 0.18)
    return jnp.clip(spiked(array, jax.random.fold_in(rng, 3), *heavy), -limit, limit).astype(held_as)


def setup_inputs(seed: int = 0) -> dict:
    keys = jax.random.split(jax.random.key(seed), 6)
    return {
        "tokens": noise_with(keys[0], (TOKENS, D), 1.0, 24.0, ((0, 512),), (0, 1, 512, 6.0), jnp.float32),
        "block_experts": draw_block_experts(jax.random.fold_in(keys[5], 71), 0),
        "weight_up": noise(keys[2], (EXPERTS, D, FF), D ** -0.5, 0.1875, ((0, 64), (2, 2))),
        "weight_down": noise(keys[3], (EXPERTS, FF, D), FF ** -0.5, 0.125, ((0, 64), (1, 2))),
        "upstream": noise_with(keys[4], (TOKENS, D), 1.0, 24.0, ((0, 512),), (0, 1, 512, 6.0), jnp.float32),
    }


def reference(tokens, block_experts, weight_up, weight_down, upstream):
    groups = N_DP
    sources = N_EXPERT
    span = BLOCK * D
    tokens_lo = tokens.astype(jnp.bfloat16)
    upstream_lo = upstream.astype(jnp.bfloat16)
    token_blocks = tokens_lo.astype(jnp.float32).reshape(groups, sources, BLOCKS_DEV, span)
    upstream_blocks = upstream_lo.astype(jnp.float32).reshape(groups, sources, BLOCKS_DEV, span)
    labels = block_experts[:, 0].reshape(groups, sources, BLOCKS_DEV)
    matches = labels[..., :, None] == labels[..., None, :]
    order = jnp.arange(BLOCKS_DEV, dtype=jnp.int32)
    earlier = order[None, :] < order[:, None]
    block_rank = lax.optimization_barrier(jnp.sum(jnp.logical_and(matches, earlier).astype(jnp.int32), axis=-1))
    slot_index = jnp.arange(CAP, dtype=jnp.int32)
    row_count = sources * CAP * BLOCK

    def expert_step(carry, expert):
        output_acc, grad_acc = carry
        chosen = jnp.logical_and((labels == expert)[..., None], block_rank[..., None] == slot_index).astype(jnp.float32)
        routed_lo = jnp.einsum('gsbc,gsbk->gsck', chosen, token_blocks, precision=lax.Precision.HIGHEST)
        routed_lo = routed_lo.astype(jnp.bfloat16).reshape(groups * row_count, D)
        routed_up = jnp.einsum('gsbc,gsbk->gsck', chosen, upstream_blocks, precision=lax.Precision.HIGHEST)
        routed_up = routed_up.astype(jnp.bfloat16).reshape(groups * row_count, D)
        up_matrix = weight_up[expert]
        down_matrix = weight_down[expert]
        pre_act = jnp.dot(routed_lo, up_matrix, preferred_element_type=jnp.float32)
        hidden = jax.nn.gelu(pre_act).astype(jnp.bfloat16)
        mixed = jnp.dot(hidden, down_matrix, preferred_element_type=jnp.float32)
        hidden_grad = jnp.dot(routed_up, down_matrix.T, preferred_element_type=jnp.float32)
        unused, gelu_back = jax.vjp(jax.nn.gelu, pre_act)
        pre_grad = gelu_back(hidden_grad)[0].astype(jnp.bfloat16)
        token_grad = jnp.dot(pre_grad, up_matrix.T, preferred_element_type=jnp.float32)
        output_acc = output_acc + jnp.einsum('gsbc,gsck->gsbk', chosen, mixed.reshape(groups, sources, CAP, span), precision=lax.Precision.HIGHEST)
        grad_acc = grad_acc + jnp.einsum('gsbc,gsck->gsbk', chosen, token_grad.reshape(groups, sources, CAP, span), precision=lax.Precision.HIGHEST)
        up_part = jnp.einsum('grk,grf->gkf', routed_lo.reshape(groups, row_count, D).astype(jnp.float32), pre_grad.reshape(groups, row_count, FF).astype(jnp.float32))
        down_part = jnp.einsum('grf,grk->gfk', hidden.reshape(groups, row_count, FF).astype(jnp.float32), routed_up.reshape(groups, row_count, D).astype(jnp.float32))
        up_total = lax.optimization_barrier(jnp.sum(lax.optimization_barrier(up_part.astype(jnp.bfloat16)).astype(jnp.float32), axis=0))
        down_total = lax.optimization_barrier(jnp.sum(lax.optimization_barrier(down_part.astype(jnp.bfloat16)).astype(jnp.float32), axis=0))
        return ((output_acc, grad_acc), (up_total, down_total))
    zeros_init = jnp.zeros((groups, sources, BLOCKS_DEV, span), jnp.float32)
    finals, grads = lax.scan(expert_step, (zeros_init, zeros_init), jnp.arange(EXPERTS, dtype=jnp.int32))
    layer_output = tokens + finals[0].reshape(TOKENS, D)
    grad_tokens = upstream + finals[1].reshape(TOKENS, D)
    return (layer_output, grad_tokens, grads[0], grads[1])
```

```python
import functools

import jax
import jax.numpy as jnp
from jax import lax
from jax.experimental import pallas as pl
from jax.experimental.pallas import tpu as pltpu
from jax.sharding import PartitionSpec as P

F32 = jnp.float32
BF16 = jnp.bfloat16
GELU_C = 0.7978845608028654
GELU_A = 0.044715
NN = (((1,), (0,)), ((), ()))
NT = (((1,), (1,)), ((), ()))
TN = (((0,), (0,)), ((), ()))


def iota(shape, axis):
    return lax.broadcasted_iota(jnp.int32, shape, axis)


def mm(a, b, dims):
    return lax.dot_general(a, b, dims, preferred_element_type=F32)


def label_column(labels):
    blocks = labels.shape[1]
    eye = iota((blocks, blocks), 0) == iota((blocks, blocks), 1)
    return jnp.sum(jnp.where(eye, labels, 0), axis=1, keepdims=True)


def slots_kernel(block, m_ref, labels_ref, tok_ref, up_ref, out_ref):
    rows = tok_ref.shape[0]
    blocks = labels_ref.shape[1]
    column = label_column(labels_ref[...])
    spread = iota((blocks, rows), 1) // block == iota((blocks, rows), 0)
    label_row = jnp.sum(jnp.where(spread, column, 0), axis=0, keepdims=True)
    dest = label_row * (2 * block) + iota((1, rows), 1) % block
    out_rows = iota((out_ref.shape[0], rows), 0)
    pick_tok = (out_rows == dest).astype(F32).astype(BF16)
    pick_up = (out_rows == dest + block).astype(F32).astype(BF16)
    total = mm(pick_tok, tok_ref[...].astype(BF16), NN)
    total = total + mm(pick_up, up_ref[...].astype(BF16), NN)
    out_ref[...] = total.astype(BF16)


def split_rows(rows, block):
    half = rows // 2
    i = iota((rows, rows), 0)
    j = lax.rem(i, half)
    source = (j // block) * (2 * block) + lax.rem(j, block) + jnp.where(i >= half, block, 0)
    return (iota((rows, rows), 1) == source).astype(F32).astype(BF16)


def merge_rows(rows, block):
    half = rows // 2
    i = iota((rows, rows), 1)
    j = lax.rem(i, half)
    source = (j // block) * (2 * block) + lax.rem(j, block) + jnp.where(i >= half, block, 0)
    return (iota((rows, rows), 0) == source).astype(F32).astype(BF16)


def grads_kernel(block, m_ref, mine_ref, other_ref, up_ref, down_ref, part_ref, hid_ref, pg_ref, x_ref):
    rows, half_cols = mine_ref.shape
    half = rows // 2
    step = pl.program_id(0)

    @pl.when(step == 0)
    def _():
        first = m_ref[0] == 0
        perm = split_rows(rows, block)
        mine = mm(perm, mine_ref[...], NN).astype(BF16)
        other = mm(perm, other_ref[...], NN).astype(BF16)
        x_ref[:, :half_cols] = jnp.where(first, mine, other)
        x_ref[:, half_cols:] = jnp.where(first, other, mine)
        pre = mm(x_ref[:half, :], up_ref[...], NN)
        hidden_grad = mm(x_ref[half:, :], down_ref[...], NT)
        square = pre * pre
        t = jnp.tanh(GELU_C * (pre + GELU_A * (square * pre)))
        cdf = 0.5 * (1.0 + t)
        slope = cdf + 0.5 * pre * (1.0 - t * t) * (GELU_C * (1.0 + 3.0 * GELU_A * square))
        hid_ref[...] = (pre * cdf).astype(BF16)
        pg_ref[...] = (hidden_grad * slope).astype(BF16)

    share = part_ref.shape[0] // 2
    cols = pl.ds(pl.multiple_of(step * share, share), share)
    part_ref[:share, :] = mm(x_ref[:half, cols], pg_ref[...], TN).astype(BF16)
    part_ref[share:, :] = mm(x_ref[half:, cols], hid_ref[...], TN).astype(BF16)


def returns_kernel(m_ref, hid_ref, pg_ref, up_ref, down_ref, keep_ref, send_ref):
    half = hid_ref.shape[0]
    half_cols = keep_ref.shape[1]
    first = m_ref[0] == 0
    mixed = mm(hid_ref[...], down_ref[...], NN)
    tgrad = mm(pg_ref[...], up_ref[...], NT)
    for k, value in ((0, mixed), (1, tgrad)):
        low, high = value[:, :half_cols], value[:, half_cols:]
        at = slice(k * half, (k + 1) * half)
        keep_ref[at, :] = jnp.where(first, low, high)
        send_ref[at, :] = jnp.where(first, high, low).astype(BF16)


def add_kernel(block, keep_ref, got_ref, out_ref):
    total = (keep_ref[...] + got_ref[...].astype(F32)).astype(BF16)
    out_ref[...] = mm(merge_rows(total.shape[0], block), total, NN).astype(BF16)


def home_kernel(block, labels_ref, back_ref, out_ref):
    rows = out_ref.shape[0] // 2
    blocks = labels_ref.shape[1]
    spread = iota((rows, blocks), 0) // block == iota((rows, blocks), 1)
    label = jnp.sum(jnp.where(spread, labels_ref[...], 0), axis=1, keepdims=True)
    dest = label * (2 * block) + iota((rows, 1), 0) % block
    columns = iota((rows, back_ref.shape[0]), 1)
    back = back_ref[...]
    for k in range(2):
        pick = (columns == dest + k * block).astype(F32).astype(BF16)
        out_ref[k * rows : (k + 1) * rows, :] = mm(pick, back, NN).astype(BF16)


def final_kernel(m_ref, mine_ref, other_ref, tok_ref, up_ref, out_ref, grad_ref):
    rows = tok_ref.shape[0]
    half_cols = mine_ref.shape[1]
    first = m_ref[0] == 0
    mine = mine_ref[...].astype(F32)
    other = other_ref[...].astype(F32)
    low = jnp.where(first, mine, other)
    high = jnp.where(first, other, mine)
    out_ref[:, :half_cols] = tok_ref[:, :half_cols] + low[:rows]
    out_ref[:, half_cols:] = tok_ref[:, half_cols:] + high[:rows]
    grad_ref[:, :half_cols] = up_ref[:, :half_cols] + low[rows:]
    grad_ref[:, half_cols:] = up_ref[:, half_cols:] + high[rows:]


def unpack_kernel(part_ref, up_ref, down_ref):
    share = up_ref.shape[0]
    up_ref[...] = part_ref[:share, :].astype(F32)
    down_ref[...] = part_ref[share:, :].astype(F32).T


def call(kernel, outs, scalars, name):
    one = not isinstance(outs, tuple)
    specs = [pl.BlockSpec(memory_space=pltpu.VMEM)]

    def run(*args):
        arrays = args[scalars:]
        return pl.pallas_call(
            kernel,
            out_shape=outs,
            in_specs=[pl.BlockSpec(memory_space=pltpu.SMEM)] * scalars + specs * len(arrays),
            out_specs=specs[0] if one else tuple(specs * len(outs)),
            name=name,
        )(*args)

    return run


def shape(dims, dtype):
    return jax.ShapeDtypeStruct(dims, dtype)


def body(tokens, block_experts, weight_up, weight_down, upstream):
    experts = lax.axis_size("expert")
    groups = lax.axis_size("dp")
    blocks_dev = block_experts.shape[0]
    tok_rows, width = tokens.shape
    block = tok_rows // blocks_dev
    half_cols = width // 2
    hidden_cols = weight_up.shape[2]
    slot_rows = experts * block
    rows = 2 * slot_rows
    share = width // groups
    m = lax.axis_index("mp").astype(jnp.int32).reshape(1)
    labels = block_experts.reshape(1, blocks_dev)
    swap = [(0, 1), (1, 0)]

    def exchange(value):
        shaped = value.reshape(experts, 2 * block, half_cols)
        moved = lax.all_to_all(shaped, "expert", split_axis=0, concat_axis=0, tiled=True)
        return moved.reshape(rows, half_cols)

    half_spec = pl.BlockSpec((tok_rows, half_cols), lambda i, m_ref: (0, m_ref[0]))
    slots = pl.pallas_call(
        functools.partial(slots_kernel, block),
        out_shape=shape((rows, half_cols), BF16),
        grid_spec=pltpu.PrefetchScalarGridSpec(
            num_scalar_prefetch=1,
            grid=(1,),
            in_specs=[pl.BlockSpec((1, blocks_dev), lambda i, m_ref: (0, 0)), half_spec, half_spec],
            out_specs=pl.BlockSpec((rows, half_cols), lambda i, m_ref: (0, 0)),
        ),
        name="slots",
    )(m, labels, tokens, upstream)
    mine = exchange(slots)
    other = lax.ppermute(mine, "mp", swap)

    up_matrix = weight_up[0]
    down_matrix = weight_down[0]

    def whole(array):
        return pl.BlockSpec(array.shape, lambda i, m_ref: (0, 0))

    half_shape = shape((slot_rows, hidden_cols), BF16)
    parts, hidden, pre_grad = pl.pallas_call(
        functools.partial(grads_kernel, block),
        out_shape=(shape((2 * width, hidden_cols), BF16), half_shape, half_shape),
        grid_spec=pltpu.PrefetchScalarGridSpec(
            num_scalar_prefetch=1,
            grid=(groups,),
            in_specs=[whole(mine), whole(other), whole(up_matrix), whole(down_matrix)],
            out_specs=(
                pl.BlockSpec((2 * share, hidden_cols), lambda i, m_ref: (i, 0)),
                whole(half_shape),
                whole(half_shape),
            ),
            scratch_shapes=[pltpu.VMEM((rows, width), BF16)],
        ),
        name="grads",
    )(m, mine, other, up_matrix, down_matrix)
    summed = lax.psum_scatter(parts, "dp", scatter_dimension=0, tiled=True)

    keep, send = call(
        returns_kernel, (shape((rows, half_cols), F32), shape((rows, half_cols), BF16)), 1, "returns"
    )(m, hidden, pre_grad, up_matrix, down_matrix)
    got = lax.ppermute(send, "mp", swap)
    added = call(functools.partial(add_kernel, block), shape((rows, half_cols), BF16), 0, "add")(keep, got)
    back = exchange(added)
    home = call(functools.partial(home_kernel, block), shape((2 * tok_rows, half_cols), BF16), 0, "home")(
        labels, back
    )
    home_other = lax.ppermute(home, "mp", swap)
    layer_output, grad_tokens = call(
        final_kernel, (shape(tokens.shape, F32), shape(tokens.shape, F32)), 1, "final"
    )(m, home, home_other, tokens, upstream)
    grad_up, grad_down = call(
        unpack_kernel, (shape((share, hidden_cols), F32), shape((hidden_cols, share), F32)), 0, "unpack"
    )(summed)
    return (layer_output, grad_tokens, grad_up[None], grad_down[None])


def solution(mesh):
    placed = (
        P(("dp", "expert"), None),
        P(("dp", "expert"), None),
        P("expert", None, "mp"),
        P("expert", "mp", None),
        P(("dp", "expert"), None),
    )
    return jax.shard_map(
        body,
        mesh=mesh,
        in_specs=placed,
        out_specs=(
            P(("dp", "expert"), None),
            P(("dp", "expert"), None),
            P("expert", "dp", "mp"),
            P("expert", "mp", "dp"),
        ),
        check_vma=False,
    )
```

```python
import functools

import jax
import jax.numpy as jnp
from jax import lax
from jax.experimental import pallas as pl
from jax.experimental.pallas import tpu as pltpu
from jax.sharding import PartitionSpec as P

F32 = jnp.float32
BF16 = jnp.bfloat16
GELU_C = 0.7978845608028654
GELU_A = 0.044715
NN = (((1,), (0,)), ((), ()))
NT = (((1,), (1,)), ((), ()))
TN = (((0,), (0,)), ((), ()))


def iota(shape, axis):
    return lax.broadcasted_iota(jnp.int32, shape, axis)


def mm(a, b, dims):
    return lax.dot_general(a, b, dims, preferred_element_type=F32)


def label_column(labels):
    blocks = labels.shape[1]
    eye = iota((blocks, blocks), 0) == iota((blocks, blocks), 1)
    return jnp.sum(jnp.where(eye, labels, 0), axis=1, keepdims=True)


def slots_kernel(block, m_ref, labels_ref, tok_ref, up_ref, out_ref):
    rows = tok_ref.shape[0]
    blocks = labels_ref.shape[1]
    column = label_column(labels_ref[...])
    spread = iota((blocks, rows), 1) // block == iota((blocks, rows), 0)
    label_row = jnp.sum(jnp.where(spread, column, 0), axis=0, keepdims=True)
    dest = label_row * (2 * block) + iota((1, rows), 1) % block
    out_rows = iota((out_ref.shape[0], rows), 0)
    pick_tok = (out_rows == dest).astype(F32).astype(BF16)
    pick_up = (out_rows == dest + block).astype(F32).astype(BF16)
    total = mm(pick_tok, tok_ref[...].astype(BF16), NN)
    total = total + mm(pick_up, up_ref[...].astype(BF16), NN)
    out_ref[...] = total.astype(BF16)


def split_rows(rows, block):
    half = rows // 2
    i = iota((rows, rows), 0)
    j = lax.rem(i, half)
    source = (j // block) * (2 * block) + lax.rem(j, block) + jnp.where(i >= half, block, 0)
    return (iota((rows, rows), 1) == source).astype(F32).astype(BF16)


def merge_rows(rows, block):
    half = rows // 2
    i = iota((rows, rows), 1)
    j = lax.rem(i, half)
    source = (j // block) * (2 * block) + lax.rem(j, block) + jnp.where(i >= half, block, 0)
    return (iota((rows, rows), 0) == source).astype(F32).astype(BF16)


def front_kernel(block, mine_ref, up_ref, down_ref, x_ref, up_out, down_out, sems):
    copies = [
        pltpu.make_async_copy(up_ref, up_out, sems.at[0]),
        pltpu.make_async_copy(down_ref, down_out, sems.at[1]),
    ]
    for copy in copies:
        copy.start()
    x_ref[...] = mm(split_rows(mine_ref.shape[0], block), mine_ref[...], NN).astype(BF16)
    for copy in copies:
        copy.wait()


def grads_kernel(
    block, share, m_ref, mine_ref, other_ref, up_ref, down_ref, part_ref, hid_ref, pg_ref, x_ref, hidt_ref
):
    rows, half_cols = mine_ref.shape
    half = rows // 2
    hidden_cols = hid_ref.shape[1]
    step = pl.program_id(0)

    @pl.when(step == 0)
    def _():
        first = m_ref[0] == 0
        mine = mine_ref[...]
        other = mm(split_rows(rows, block), other_ref[...], NN).astype(BF16)
        x_ref[:, :half_cols] = jnp.where(first, mine, other)
        x_ref[:, half_cols:] = jnp.where(first, other, mine)
        pre = mm(x_ref[:half, :], up_ref[...], NN)
        hidden_grad = mm(x_ref[half:, :], down_ref[...], NT)
        square = pre * pre
        t = jnp.tanh(GELU_C * (pre + GELU_A * (square * pre)))
        cdf = 0.5 * (1.0 + t)
        slope = cdf + 0.5 * pre * (1.0 - t * t) * (GELU_C * (1.0 + 3.0 * GELU_A * square))
        hidden = (pre * cdf).astype(BF16)
        hid_ref[...] = hidden
        hidt_ref[...] = hidden.T
        pg_ref[...] = (hidden_grad * slope).astype(BF16)

    shares = part_ref.shape[0] // (2 * hidden_cols)
    span = shares * share
    cols = pl.ds(pl.multiple_of(step * span, span), span)
    up_part = mm(x_ref[:half, cols], pg_ref[...], TN).astype(BF16)
    down_part = mm(hidt_ref[...], x_ref[half:, cols], NN).astype(BF16)
    for k in range(shares):
        own = slice(k * share, (k + 1) * share)
        base = 2 * k * hidden_cols
        for j in range(hidden_cols // share):
            at = slice(j * share, (j + 1) * share)
            part_ref[base + j * share : base + (j + 1) * share, :] = up_part[own, at]
        part_ref[base + hidden_cols : base + 2 * hidden_cols, :] = down_part[:, own]


def returns_kernel(m_ref, hid_ref, pg_ref, up_ref, down_ref, keep_ref, send_ref):
    half = hid_ref.shape[0]
    half_cols = keep_ref.shape[1]
    first = m_ref[0] == 0
    mixed = mm(hid_ref[...], down_ref[...], NN)
    tgrad = mm(pg_ref[...], up_ref[...], NT)
    for k, value in ((0, mixed), (1, tgrad)):
        low, high = value[:, :half_cols], value[:, half_cols:]
        at = slice(k * half, (k + 1) * half)
        keep_ref[at, :] = jnp.where(first, low, high)
        send_ref[at, :] = jnp.where(first, high, low).astype(BF16)


def add_kernel(block, keep_ref, got_ref, out_ref):
    total = (keep_ref[...] + got_ref[...].astype(F32)).astype(BF16)
    out_ref[...] = mm(merge_rows(total.shape[0], block), total, NN).astype(BF16)


def home_kernel(block, labels_ref, back_ref, out_ref):
    rows = out_ref.shape[0] // 2
    blocks = labels_ref.shape[1]
    spread = iota((rows, blocks), 0) // block == iota((rows, blocks), 1)
    label = jnp.sum(jnp.where(spread, labels_ref[...], 0), axis=1, keepdims=True)
    dest = label * (2 * block) + iota((rows, 1), 0) % block
    columns = iota((rows, back_ref.shape[0]), 1)
    back = back_ref[...]
    for k in range(2):
        pick = (columns == dest + k * block).astype(F32).astype(BF16)
        out_ref[k * rows : (k + 1) * rows, :] = mm(pick, back, NN).astype(BF16)


def final_kernel(m_ref, mine_ref, other_ref, tok_ref, up_ref, out_ref, grad_ref):
    rows = tok_ref.shape[0]
    half_cols = mine_ref.shape[1]
    first = m_ref[0] == 0
    mine = mine_ref[...].astype(F32)
    other = other_ref[...].astype(F32)
    low = jnp.where(first, mine, other)
    high = jnp.where(first, other, mine)
    out_ref[:, :half_cols] = tok_ref[:, :half_cols] + low[:rows]
    out_ref[:, half_cols:] = tok_ref[:, half_cols:] + high[:rows]
    grad_ref[:, :half_cols] = up_ref[:, :half_cols] + low[rows:]
    grad_ref[:, half_cols:] = up_ref[:, half_cols:] + high[rows:]


def unpack_kernel(part_ref, up_ref, down_ref):
    hidden_cols, share = down_ref.shape
    for j in range(hidden_cols // share):
        at = slice(j * share, (j + 1) * share)
        up_ref[:, at] = part_ref[at, :].astype(F32)
    down_ref[...] = part_ref[hidden_cols:, :].astype(F32)


PARAMS = pltpu.CompilerParams(vmem_limit_bytes=20 * 2**20)
ONCHIP = pl.BlockSpec(memory_space=pltpu.VMEM)


def onchip(array):
    return pltpu.with_memory_space_constraint(array, pltpu.VMEM)


def offchip(array):
    return pltpu.with_memory_space_constraint(array, pltpu.HBM)


def call(kernel, outs, scalars, name):
    one = not isinstance(outs, tuple)

    def run(*args):
        arrays = len(args) - scalars
        return pl.pallas_call(
            kernel,
            out_shape=outs,
            in_specs=[pl.BlockSpec(memory_space=pltpu.SMEM)] * scalars + [ONCHIP] * arrays,
            out_specs=ONCHIP if one else (ONCHIP,) * len(outs),
            compiler_params=PARAMS,
            name=name,
        )(*args)

    return run


def shape(dims, dtype):
    return jax.ShapeDtypeStruct(dims, dtype)


def slots_call(block, rows, m, labels, tokens, upstream):
    tok_rows, width = tokens.shape
    half_spec = pl.BlockSpec((tok_rows, width // 2), lambda i, m_ref: (0, m_ref[0]))
    return pl.pallas_call(
        functools.partial(slots_kernel, block),
        out_shape=pltpu.VMEM((rows, width // 2), BF16),
        grid_spec=pltpu.PrefetchScalarGridSpec(
            num_scalar_prefetch=1,
            grid=(1,),
            in_specs=[pl.BlockSpec(labels.shape, lambda i, m_ref: (0, 0)), half_spec, half_spec],
            out_specs=ONCHIP,
        ),
        compiler_params=PARAMS,
        name="slots",
    )(m, offchip(labels), offchip(tokens), offchip(upstream))


def front_call(block, mine, up_matrix, down_matrix):
    anywhere = pl.BlockSpec(memory_space=pl.ANY)
    return pl.pallas_call(
        functools.partial(front_kernel, block),
        out_shape=(
            pltpu.VMEM(mine.shape, BF16),
            pltpu.VMEM(up_matrix.shape, BF16),
            pltpu.VMEM(down_matrix.shape, BF16),
        ),
        in_specs=[ONCHIP, anywhere, anywhere],
        out_specs=(ONCHIP, ONCHIP, ONCHIP),
        scratch_shapes=[pltpu.SemaphoreType.DMA((2,))],
        compiler_params=PARAMS,
        name="front",
    )(onchip(mine), offchip(up_matrix), offchip(down_matrix))


def grads_call(block, groups, m, mine, other, up_matrix, down_matrix):
    rows = mine.shape[0]
    width, hidden_cols = up_matrix.shape
    share = width // groups
    steps = max(1, groups // 4)
    half_shape = pltpu.VMEM((rows // 2, hidden_cols), BF16)
    return pl.pallas_call(
        functools.partial(grads_kernel, block, share),
        out_shape=(pltpu.HBM((2 * hidden_cols * groups, share), BF16), half_shape, half_shape),
        grid_spec=pltpu.PrefetchScalarGridSpec(
            num_scalar_prefetch=1,
            grid=(steps,),
            in_specs=[ONCHIP] * 4,
            out_specs=(
                pl.BlockSpec((2 * hidden_cols * groups // steps, share), lambda i, m_ref: (i, 0)),
                ONCHIP,
                ONCHIP,
            ),
            scratch_shapes=[pltpu.VMEM((rows, width), BF16), pltpu.VMEM((hidden_cols, rows // 2), BF16)],
        ),
        compiler_params=PARAMS,
        name="grads",
    )(m, onchip(mine), onchip(other), onchip(up_matrix), onchip(down_matrix))


def body(tokens, block_experts, weight_up, weight_down, upstream):
    experts = lax.axis_size("expert")
    groups = lax.axis_size("dp")
    blocks_dev = block_experts.shape[0]
    tok_rows, width = tokens.shape
    block = tok_rows // blocks_dev
    half_cols = width // 2
    hidden_cols = weight_up.shape[2]
    rows = 2 * experts * block
    share = width // groups
    m = lax.axis_index("mp").astype(jnp.int32).reshape(1)
    labels = block_experts.reshape(1, blocks_dev)
    swap = [(0, 1), (1, 0)]

    def exchange(value):
        shaped = value.reshape(experts, 2 * block, half_cols)
        moved = lax.all_to_all(shaped, "expert", split_axis=0, concat_axis=0, tiled=True)
        return moved.reshape(rows, half_cols)

    slots = slots_call(block, rows, m, labels, tokens, upstream)
    arrived = exchange(slots)
    other = lax.ppermute(arrived, "mp", swap)
    mine, up_matrix, down_matrix = front_call(block, arrived, weight_up[0], weight_down[0])
    parts, hidden, pre_grad = grads_call(block, groups, m, mine, other, up_matrix, down_matrix)
    summed = lax.psum_scatter(parts, "dp", scatter_dimension=0, tiled=True)

    keep, send = call(
        returns_kernel, (pltpu.VMEM((rows, half_cols), F32), pltpu.VMEM((rows, half_cols), BF16)), 1, "returns"
    )(m, onchip(hidden), onchip(pre_grad), weight_up[0], weight_down[0])
    got = lax.ppermute(send, "mp", swap)
    added = call(functools.partial(add_kernel, block), pltpu.VMEM((rows, half_cols), BF16), 0, "add")(
        onchip(keep), onchip(got)
    )
    back = exchange(added)
    home = call(functools.partial(home_kernel, block), pltpu.VMEM((2 * tok_rows, half_cols), BF16), 0, "home")(
        labels, onchip(back)
    )
    home_other = lax.ppermute(home, "mp", swap)
    layer_output, grad_tokens = call(
        final_kernel, (shape(tokens.shape, F32), shape(tokens.shape, F32)), 1, "final"
    )(m, onchip(home), onchip(home_other), tokens, upstream)
    grad_up, grad_down = call(
        unpack_kernel, (shape((share, hidden_cols), F32), shape((hidden_cols, share), F32)), 0, "unpack"
    )(offchip(summed))
    return (layer_output, grad_tokens, grad_up[None], grad_down[None])


def solution(mesh):
    placed = (
        P(("dp", "expert"), None),
        P(("dp", "expert"), None),
        P("expert", None, "mp"),
        P("expert", "mp", None),
        P(("dp", "expert"), None),
    )
    return jax.shard_map(
        body,
        mesh=mesh,
        in_specs=placed,
        out_specs=(
            P(("dp", "expert"), None),
            P(("dp", "expert"), None),
            P("expert", "dp", "mp"),
            P("expert", "mp", "dp"),
        ),
        check_vma=False,
    )
```

```python
import functools

import jax
import jax.numpy as jnp
from jax import lax
from jax.experimental import pallas as pl
from jax.experimental.pallas import tpu as pltpu
from jax.sharding import PartitionSpec as P

F32 = jnp.float32
BF16 = jnp.bfloat16
GELU_C = 0.7978845608028654
GELU_A = 0.044715
NN = (((1,), (0,)), ((), ()))
NT = (((1,), (1,)), ((), ()))
TN = (((0,), (0,)), ((), ()))


def iota(shape, axis):
    return lax.broadcasted_iota(jnp.int32, shape, axis)


def mm(a, b, dims):
    return lax.dot_general(a, b, dims, preferred_element_type=F32)


def label_column(labels):
    blocks = labels.shape[1]
    eye = iota((blocks, blocks), 0) == iota((blocks, blocks), 1)
    return jnp.sum(jnp.where(eye, labels, 0), axis=1, keepdims=True)


def slots_kernel(block, m_ref, labels_ref, tok_ref, up_ref, out_ref):
    rows = tok_ref.shape[0]
    blocks = labels_ref.shape[1]
    column = label_column(labels_ref[...])
    spread = iota((blocks, rows), 1) // block == iota((blocks, rows), 0)
    label_row = jnp.sum(jnp.where(spread, column, 0), axis=0, keepdims=True)
    dest = label_row * (2 * block) + iota((1, rows), 1) % block
    out_rows = iota((out_ref.shape[0], rows), 0)
    pick_tok = (out_rows == dest).astype(F32).astype(BF16)
    pick_up = (out_rows == dest + block).astype(F32).astype(BF16)
    total = mm(pick_tok, tok_ref[...].astype(BF16), NN)
    total = total + mm(pick_up, up_ref[...].astype(BF16), NN)
    out_ref[...] = total.astype(BF16)


def split_rows(rows, block):
    half = rows // 2
    i = iota((rows, rows), 0)
    j = lax.rem(i, half)
    source = (j // block) * (2 * block) + lax.rem(j, block) + jnp.where(i >= half, block, 0)
    return (iota((rows, rows), 1) == source).astype(F32).astype(BF16)


def merge_rows(rows, block):
    half = rows // 2
    i = iota((rows, rows), 1)
    j = lax.rem(i, half)
    source = (j // block) * (2 * block) + lax.rem(j, block) + jnp.where(i >= half, block, 0)
    return (iota((rows, rows), 0) == source).astype(F32).astype(BF16)


def front_kernel(block, mine_ref, up_ref, down_ref, x_ref, up_out, down_out, sems):
    copies = [
        pltpu.make_async_copy(up_ref, up_out, sems.at[0]),
        pltpu.make_async_copy(down_ref, down_out, sems.at[1]),
    ]
    for copy in copies:
        copy.start()
    x_ref[...] = mm(split_rows(mine_ref.shape[0], block), mine_ref[...], NN).astype(BF16)
    for copy in copies:
        copy.wait()


def hidden_kernel(
    block, groups, m_ref, group_ref, mine_ref, other_ref, up_ref, down_ref,
    far_up_ref, far_down_ref, hid_ref, pg_ref, turned_ref, hidt_ref, x_ref,
):
    rows, half_cols = mine_ref.shape
    half = rows // 2
    share = turned_ref.shape[1] // groups
    first = m_ref[0] == 0
    mine = mine_ref[...]
    other = mm(split_rows(rows, block), other_ref[...], NN).astype(BF16)
    x_ref[:, :half_cols] = jnp.where(first, mine, other)
    x_ref[:, half_cols:] = jnp.where(first, other, mine)
    for k in range(groups):
        owner = lax.rem(group_ref[0] + k, groups)
        turned_ref[:, k * share : (k + 1) * share] = x_ref[:, pl.ds(pl.multiple_of(owner * share, share), share)]
    pre = mm(x_ref[:half, :], up_ref[...], NN)
    hidden_grad = mm(x_ref[half:, :], down_ref[...], NT)
    square = pre * pre
    t = jnp.tanh(GELU_C * (pre + GELU_A * (square * pre)))
    cdf = 0.5 * (1.0 + t)
    slope = cdf + 0.5 * pre * (1.0 - t * t) * (GELU_C * (1.0 + 3.0 * GELU_A * square))
    hidden = (pre * cdf).astype(BF16)
    hid_ref[...] = hidden
    hidt_ref[...] = hidden.T
    pg_ref[...] = (hidden_grad * slope).astype(BF16)
    far = slice(groups // 2 * share, (groups // 2 + 1) * share)
    up_share(far_up_ref, 0, mm(turned_ref[:half, far], pg_ref[...], TN).astype(BF16))
    far_down_ref[...] = mm(hidt_ref[...], turned_ref[half:, far], NN).astype(BF16)


def up_share(ref, base, value):
    share = value.shape[0]
    for j in range(value.shape[1] // share):
        ref[base + j * share : base + (j + 1) * share, :] = value[:, j * share : (j + 1) * share]


def shares_kernel(slots, turned_ref, hidt_ref, pg_ref, *part_refs):
    half = pg_ref.shape[0]
    hidden_cols, share = hidt_ref.shape[0], part_refs[0].shape[1]
    done = 0
    for first, last in slots:
        cols = slice(first * share, last * share)
        up_part = mm(turned_ref[:half, cols], pg_ref[...], TN).astype(BF16)
        down_part = mm(hidt_ref[...], turned_ref[half:, cols], NN).astype(BF16)
        for k in range(last - first):
            own = slice(k * share, (k + 1) * share)
            up_share(part_refs[done], 0, up_part[own, :])
            part_refs[done][hidden_cols:, :] = down_part[:, own]
            done += 1


def hop_kernel(lower, got_ref, part_ref, out_ref):
    half = out_ref.shape[0] // 2
    if lower is None:
        out_ref[...] = (part_ref[...].astype(F32) + got_ref[...].astype(F32)).astype(BF16)
        return
    came = slice(half, 2 * half) if lower else slice(0, half)
    fresh = slice(0, half) if lower else slice(half, 2 * half)
    out_ref[came, :] = (part_ref[came, :].astype(F32) + got_ref[...].astype(F32)).astype(BF16)
    out_ref[fresh, :] = part_ref[fresh, :]


def last_kernel(left_ref, right_ref, part_ref, up_ref, down_ref):
    hidden_cols, share = down_ref.shape

    def total(at):
        return part_ref[at, :].astype(F32) + (left_ref[at, :].astype(F32) + right_ref[at, :].astype(F32))

    for j in range(hidden_cols // share):
        at = slice(j * share, (j + 1) * share)
        up_ref[:, at] = total(at)
    down_ref[...] = total(slice(hidden_cols, 2 * hidden_cols))


def returns_kernel(m_ref, hid_ref, pg_ref, up_ref, down_ref, keep_ref, send_ref):
    half = hid_ref.shape[0]
    half_cols = keep_ref.shape[1]
    first = m_ref[0] == 0
    mixed = mm(hid_ref[...], down_ref[...], NN)
    tgrad = mm(pg_ref[...], up_ref[...], NT)
    for k, value in ((0, mixed), (1, tgrad)):
        low, high = value[:, :half_cols], value[:, half_cols:]
        at = slice(k * half, (k + 1) * half)
        keep_ref[at, :] = jnp.where(first, low, high)
        send_ref[at, :] = jnp.where(first, high, low).astype(BF16)


def add_kernel(block, keep_ref, got_ref, out_ref):
    total = (keep_ref[...] + got_ref[...].astype(F32)).astype(BF16)
    out_ref[...] = mm(merge_rows(total.shape[0], block), total, NN).astype(BF16)


def home_kernel(block, labels_ref, back_ref, out_ref):
    rows = out_ref.shape[0] // 2
    blocks = labels_ref.shape[1]
    spread = iota((rows, blocks), 0) // block == iota((rows, blocks), 1)
    label = jnp.sum(jnp.where(spread, labels_ref[...], 0), axis=1, keepdims=True)
    dest = label * (2 * block) + iota((rows, 1), 0) % block
    columns = iota((rows, back_ref.shape[0]), 1)
    back = back_ref[...]
    for k in range(2):
        pick = (columns == dest + k * block).astype(F32).astype(BF16)
        out_ref[k * rows : (k + 1) * rows, :] = mm(pick, back, NN).astype(BF16)


def final_kernel(m_ref, mine_ref, other_ref, tok_ref, up_ref, out_ref, grad_ref):
    rows = tok_ref.shape[0]
    half_cols = mine_ref.shape[1]
    first = m_ref[0] == 0
    mine = mine_ref[...].astype(F32)
    other = other_ref[...].astype(F32)
    low = jnp.where(first, mine, other)
    high = jnp.where(first, other, mine)
    out_ref[:, :half_cols] = tok_ref[:, :half_cols] + low[:rows]
    out_ref[:, half_cols:] = tok_ref[:, half_cols:] + high[:rows]
    grad_ref[:, :half_cols] = up_ref[:, :half_cols] + low[rows:]
    grad_ref[:, half_cols:] = up_ref[:, half_cols:] + high[rows:]


PARAMS = pltpu.CompilerParams(vmem_limit_bytes=16 * 2**20)
ONCHIP = pl.BlockSpec(memory_space=pltpu.VMEM)


def onchip(array):
    return pltpu.with_memory_space_constraint(array, pltpu.VMEM)


def offchip(array):
    return pltpu.with_memory_space_constraint(array, pltpu.HBM)


def call(kernel, outs, scalars, name):
    one = not isinstance(outs, tuple)

    def run(*args):
        arrays = len(args) - scalars
        return pl.pallas_call(
            kernel,
            out_shape=outs,
            in_specs=[pl.BlockSpec(memory_space=pltpu.SMEM)] * scalars + [ONCHIP] * arrays,
            out_specs=ONCHIP if one else (ONCHIP,) * len(outs),
            compiler_params=PARAMS,
            name=name,
        )(*args)

    return run


def shape(dims, dtype):
    return jax.ShapeDtypeStruct(dims, dtype)


def slots_call(block, rows, m, labels, tokens, upstream):
    tok_rows, width = tokens.shape
    half_spec = pl.BlockSpec((tok_rows, width // 2), lambda i, m_ref: (0, m_ref[0]))
    return pl.pallas_call(
        functools.partial(slots_kernel, block),
        out_shape=pltpu.VMEM((rows, width // 2), BF16),
        grid_spec=pltpu.PrefetchScalarGridSpec(
            num_scalar_prefetch=1,
            grid=(1,),
            in_specs=[pl.BlockSpec(labels.shape, lambda i, m_ref: (0, 0)), half_spec, half_spec],
            out_specs=ONCHIP,
        ),
        compiler_params=PARAMS,
        name="slots",
    )(m, offchip(labels), offchip(tokens), offchip(upstream))


def front_call(block, mine, up_matrix, down_matrix):
    anywhere = pl.BlockSpec(memory_space=pl.ANY)
    return pl.pallas_call(
        functools.partial(front_kernel, block),
        out_shape=(
            pltpu.VMEM(mine.shape, BF16),
            pltpu.VMEM(up_matrix.shape, BF16),
            pltpu.VMEM(down_matrix.shape, BF16),
        ),
        in_specs=[ONCHIP, anywhere, anywhere],
        out_specs=(ONCHIP, ONCHIP, ONCHIP),
        scratch_shapes=[pltpu.SemaphoreType.DMA((2,))],
        compiler_params=PARAMS,
        name="front",
    )(onchip(mine), offchip(up_matrix), offchip(down_matrix))


def weight_grads(block, groups, m, group, mine, other, up_matrix, down_matrix):
    rows = mine.shape[0]
    width, hidden_cols = up_matrix.shape
    share = width // groups
    half = groups // 2
    vmem = pltpu.VMEM
    far_up, far_down, hidden, pre_grad, turned, hidden_t = pl.pallas_call(
        functools.partial(hidden_kernel, block, groups),
        out_shape=(
            vmem((hidden_cols, share), BF16),
            vmem((hidden_cols, share), BF16),
            vmem((rows // 2, hidden_cols), BF16),
            vmem((rows // 2, hidden_cols), BF16),
            vmem((rows, width), BF16),
            vmem((hidden_cols, rows // 2), BF16),
        ),
        in_specs=[pl.BlockSpec(memory_space=pltpu.SMEM)] * 2 + [ONCHIP] * 4,
        out_specs=(ONCHIP,) * 6,
        scratch_shapes=[vmem((rows, width), BF16)],
        compiler_params=PARAMS,
        name="hidden",
    )(m, group, onchip(mine), onchip(other), onchip(up_matrix), onchip(down_matrix))
    ahead = [(i, (i + 1) % groups) for i in range(groups)]
    behind = [(i, (i - 1) % groups) for i in range(groups)]
    right = lax.ppermute(far_up, "dp", ahead)
    left = lax.ppermute(far_down, "dp", behind)
    size = vmem((2 * hidden_cols, share), BF16)
    runs = ((0, half), (half + 1, groups))
    parts = call(functools.partial(shares_kernel, runs), (size,) * (groups - 1), 0, "shares")(
        onchip(turned), onchip(hidden_t), onchip(pre_grad)
    )
    parts = parts[:half] + (None,) + parts[half:]
    for hop in range(half - 1, 0, -1):
        whole = hop < half - 1
        step = call(functools.partial(hop_kernel, None if whole else False), size, 0, "ahead")
        right = lax.ppermute(step(onchip(right), onchip(parts[hop])), "dp", ahead)
        step = call(functools.partial(hop_kernel, None if whole else True), size, 0, "behind")
        left = lax.ppermute(step(onchip(left), onchip(parts[groups - hop])), "dp", behind)
    grad_up, grad_down = call(
        last_kernel, (shape((share, hidden_cols), F32), shape((hidden_cols, share), F32)), 0, "last"
    )(onchip(left), onchip(right), onchip(parts[0]))
    return grad_up, grad_down, hidden, pre_grad


def body(tokens, block_experts, weight_up, weight_down, upstream):
    experts = lax.axis_size("expert")
    groups = lax.axis_size("dp")
    blocks_dev = block_experts.shape[0]
    tok_rows, width = tokens.shape
    block = tok_rows // blocks_dev
    half_cols = width // 2
    rows = 2 * experts * block
    m = lax.axis_index("mp").astype(jnp.int32).reshape(1)
    labels = block_experts.reshape(1, blocks_dev)
    swap = [(0, 1), (1, 0)]

    def exchange(value):
        shaped = value.reshape(experts, 2 * block, half_cols)
        moved = lax.all_to_all(shaped, "expert", split_axis=0, concat_axis=0, tiled=True)
        return moved.reshape(rows, half_cols)

    slots = slots_call(block, rows, m, labels, tokens, upstream)
    arrived = exchange(slots)
    other = lax.ppermute(arrived, "mp", swap)
    mine, up_matrix, down_matrix = front_call(block, arrived, weight_up[0], weight_down[0])
    group = lax.axis_index("dp").astype(jnp.int32).reshape(1)
    grad_up, grad_down, hidden, pre_grad = weight_grads(block, groups, m, group, mine, other, up_matrix, down_matrix)

    keep, send = call(
        returns_kernel, (pltpu.VMEM((rows, half_cols), F32), pltpu.VMEM((rows, half_cols), BF16)), 1, "returns"
    )(m, onchip(hidden), onchip(pre_grad), onchip(up_matrix), onchip(down_matrix))
    got = lax.ppermute(send, "mp", swap)
    added = call(functools.partial(add_kernel, block), pltpu.VMEM((rows, half_cols), BF16), 0, "add")(
        onchip(keep), onchip(got)
    )
    back = exchange(added)
    home = call(functools.partial(home_kernel, block), pltpu.VMEM((2 * tok_rows, half_cols), BF16), 0, "home")(
        labels, onchip(back)
    )
    home_other = lax.ppermute(home, "mp", swap)
    layer_output, grad_tokens = call(
        final_kernel, (shape(tokens.shape, F32), shape(tokens.shape, F32)), 1, "final"
    )(m, onchip(home), onchip(home_other), tokens, upstream)
    return (layer_output, grad_tokens, grad_up[None], grad_down[None])


def solution(mesh):
    placed = (
        P(("dp", "expert"), None),
        P(("dp", "expert"), None),
        P("expert", None, "mp"),
        P("expert", "mp", None),
        P(("dp", "expert"), None),
    )
    return jax.shard_map(
        body,
        mesh=mesh,
        in_specs=placed,
        out_specs=(
            P(("dp", "expert"), None),
            P(("dp", "expert"), None),
            P("expert", "dp", "mp"),
            P("expert", "mp", "dp"),
        ),
        check_vma=False,
    )
```

```python
import functools

import jax
import jax.numpy as jnp
from jax import lax
from jax.experimental import pallas as pl
from jax.experimental.pallas import tpu as pltpu
from jax.sharding import PartitionSpec as P

F32 = jnp.float32
BF16 = jnp.bfloat16
GELU_C = 0.7978845608028654
GELU_A = 0.044715
NN = (((1,), (0,)), ((), ()))
NT = (((1,), (1,)), ((), ()))
TN = (((0,), (0,)), ((), ()))


def iota(shape, axis):
    return lax.broadcasted_iota(jnp.int32, shape, axis)


def mm(a, b, dims):
    return lax.dot_general(a, b, dims, preferred_element_type=F32)


def label_column(labels):
    blocks = labels.shape[1]
    eye = iota((blocks, blocks), 0) == iota((blocks, blocks), 1)
    return jnp.sum(jnp.where(eye, labels, 0), axis=1, keepdims=True)


def slots_kernel(block, m_ref, labels_ref, tok_ref, up_ref, out_ref):
    rows = tok_ref.shape[0]
    blocks = labels_ref.shape[1]
    column = label_column(labels_ref[...])
    spread = iota((blocks, rows), 1) // block == iota((blocks, rows), 0)
    label_row = jnp.sum(jnp.where(spread, column, 0), axis=0, keepdims=True)
    dest = label_row * (2 * block) + iota((1, rows), 1) % block
    out_rows = iota((out_ref.shape[0], rows), 0)
    pick_tok = (out_rows == dest).astype(F32).astype(BF16)
    pick_up = (out_rows == dest + block).astype(F32).astype(BF16)
    total = mm(pick_tok, tok_ref[...].astype(BF16), NN)
    total = total + mm(pick_up, up_ref[...].astype(BF16), NN)
    out_ref[...] = total.astype(BF16)


def split_rows(rows, block):
    half = rows // 2
    i = iota((rows, rows), 0)
    j = lax.rem(i, half)
    source = (j // block) * (2 * block) + lax.rem(j, block) + jnp.where(i >= half, block, 0)
    return (iota((rows, rows), 1) == source).astype(F32).astype(BF16)


def merge_rows(rows, block):
    half = rows // 2
    i = iota((rows, rows), 1)
    j = lax.rem(i, half)
    source = (j // block) * (2 * block) + lax.rem(j, block) + jnp.where(i >= half, block, 0)
    return (iota((rows, rows), 0) == source).astype(F32).astype(BF16)


def front_kernel(block, mine_ref, up_ref, down_ref, x_ref, up_out, down_out, sems):
    copies = [
        pltpu.make_async_copy(up_ref, up_out, sems.at[0]),
        pltpu.make_async_copy(down_ref, down_out, sems.at[1]),
    ]
    for copy in copies:
        copy.start()
    x_ref[...] = mm(split_rows(mine_ref.shape[0], block), mine_ref[...], NN).astype(BF16)
    for copy in copies:
        copy.wait()


def hidden_kernel(
    block, groups, m_ref, group_ref, mine_ref, other_ref, up_ref, down_ref,
    far_up_ref, far_down_ref, hid_ref, pg_ref, turned_ref, hidt_ref, x_ref,
):
    rows, half_cols = mine_ref.shape
    half = rows // 2
    share = turned_ref.shape[1] // groups
    first = m_ref[0] == 0
    mine = mine_ref[...]
    other = mm(split_rows(rows, block), other_ref[...], NN).astype(BF16)
    x_ref[:, :half_cols] = jnp.where(first, mine, other)
    x_ref[:, half_cols:] = jnp.where(first, other, mine)
    for k in range(groups):
        owner = lax.rem(group_ref[0] + k, groups)
        turned_ref[:, k * share : (k + 1) * share] = x_ref[:, pl.ds(pl.multiple_of(owner * share, share), share)]
    pre = mm(x_ref[:half, :], up_ref[...], NN)
    hidden_grad = mm(x_ref[half:, :], down_ref[...], NT)
    square = pre * pre
    t = jnp.tanh(GELU_C * (pre + GELU_A * (square * pre)))
    cdf = 0.5 * (1.0 + t)
    slope = cdf + 0.5 * pre * (1.0 - t * t) * (GELU_C * (1.0 + 3.0 * GELU_A * square))
    hidden = (pre * cdf).astype(BF16)
    hid_ref[...] = hidden
    hidt_ref[...] = hidden.T
    pg_ref[...] = (hidden_grad * slope).astype(BF16)
    far = slice(groups // 2 * share, (groups // 2 + 1) * share)
    up_share(far_up_ref, 0, mm(turned_ref[:half, far], pg_ref[...], TN).astype(BF16))
    far_down_ref[...] = mm(hidt_ref[...], turned_ref[half:, far], NN).astype(BF16)


def up_share(ref, base, value):
    share = value.shape[0]
    for j in range(value.shape[1] // share):
        ref[base + j * share : base + (j + 1) * share, :] = value[:, j * share : (j + 1) * share]


def shares_kernel(slots, turned_ref, hidt_ref, pg_ref, *part_refs):
    half = pg_ref.shape[0]
    hidden_cols, share = hidt_ref.shape[0], part_refs[0].shape[1]
    done = 0
    for first, last in slots:
        cols = slice(first * share, last * share)
        up_part = mm(turned_ref[:half, cols], pg_ref[...], TN).astype(BF16)
        down_part = mm(hidt_ref[...], turned_ref[half:, cols], NN).astype(BF16)
        for k in range(last - first):
            own = slice(k * share, (k + 1) * share)
            up_share(part_refs[done], 0, up_part[own, :])
            part_refs[done][hidden_cols:, :] = down_part[:, own]
            done += 1


def hop_kernel(lower, got_ref, part_ref, out_ref):
    half = out_ref.shape[0] // 2
    if lower is None:
        out_ref[...] = (part_ref[...].astype(F32) + got_ref[...].astype(F32)).astype(BF16)
        return
    came = slice(half, 2 * half) if lower else slice(0, half)
    fresh = slice(0, half) if lower else slice(half, 2 * half)
    out_ref[came, :] = (part_ref[came, :].astype(F32) + got_ref[...].astype(F32)).astype(BF16)
    out_ref[fresh, :] = part_ref[fresh, :]


def last_kernel(after_ref, left_ref, right_ref, part_ref, up_ref, down_ref):
    del after_ref
    hidden_cols, share = down_ref.shape

    def total(at):
        return part_ref[at, :].astype(F32) + (left_ref[at, :].astype(F32) + right_ref[at, :].astype(F32))

    for j in range(hidden_cols // share):
        at = slice(j * share, (j + 1) * share)
        up_ref[:, at] = total(at)
    down_ref[...] = total(slice(hidden_cols, 2 * hidden_cols))


def returns_kernel(m_ref, hid_ref, pg_ref, up_ref, down_ref, keep_ref, send_ref):
    half = hid_ref.shape[0]
    half_cols = keep_ref.shape[1]
    first = m_ref[0] == 0
    mixed = mm(hid_ref[...], down_ref[...], NN)
    tgrad = mm(pg_ref[...], up_ref[...], NT)
    for k, value in ((0, mixed), (1, tgrad)):
        low, high = value[:, :half_cols], value[:, half_cols:]
        at = slice(k * half, (k + 1) * half)
        keep_ref[at, :] = jnp.where(first, low, high)
        send_ref[at, :] = jnp.where(first, high, low).astype(BF16)


def add_kernel(block, after_ref, also_ref, keep_ref, got_ref, out_ref):
    del after_ref, also_ref
    total = (keep_ref[...] + got_ref[...].astype(F32)).astype(BF16)
    out_ref[...] = mm(merge_rows(total.shape[0], block), total, NN).astype(BF16)


def home_kernel(block, labels_ref, back_ref, out_ref):
    rows = out_ref.shape[0] // 2
    blocks = labels_ref.shape[1]
    spread = iota((rows, blocks), 0) // block == iota((rows, blocks), 1)
    label = jnp.sum(jnp.where(spread, labels_ref[...], 0), axis=1, keepdims=True)
    dest = label * (2 * block) + iota((rows, 1), 0) % block
    columns = iota((rows, back_ref.shape[0]), 1)
    back = back_ref[...]
    for k in range(2):
        pick = (columns == dest + k * block).astype(F32).astype(BF16)
        out_ref[k * rows : (k + 1) * rows, :] = mm(pick, back, NN).astype(BF16)


def final_kernel(m_ref, mine_ref, other_ref, tok_ref, up_ref, out_ref, grad_ref):
    rows = tok_ref.shape[0]
    half_cols = mine_ref.shape[1]
    first = m_ref[0] == 0
    mine = mine_ref[...].astype(F32)
    other = other_ref[...].astype(F32)
    low = jnp.where(first, mine, other)
    high = jnp.where(first, other, mine)
    out_ref[:, :half_cols] = tok_ref[:, :half_cols] + low[:rows]
    out_ref[:, half_cols:] = tok_ref[:, half_cols:] + high[:rows]
    grad_ref[:, :half_cols] = up_ref[:, :half_cols] + low[rows:]
    grad_ref[:, half_cols:] = up_ref[:, half_cols:] + high[rows:]


PARAMS = pltpu.CompilerParams(vmem_limit_bytes=16 * 2**20)
def long(us):
    return pl.CostEstimate(flops=us * 1_000_000_000, bytes_accessed=us * 3_000_000, transcendentals=0)


ONCHIP = pl.BlockSpec(memory_space=pltpu.VMEM)


def onchip(array):
    return pltpu.with_memory_space_constraint(array, pltpu.VMEM)


def offchip(array):
    return pltpu.with_memory_space_constraint(array, pltpu.HBM)


def call(kernel, outs, scalars, name, after=0, cost=None):
    one = not isinstance(outs, tuple)
    unread = [pl.BlockSpec(memory_space=pl.ANY)] * after

    def run(*args):
        arrays = len(args) - scalars - after
        return pl.pallas_call(
            kernel,
            out_shape=outs,
            in_specs=[pl.BlockSpec(memory_space=pltpu.SMEM)] * scalars + unread + [ONCHIP] * arrays,
            out_specs=ONCHIP if one else (ONCHIP,) * len(outs),
            compiler_params=PARAMS,
            cost_estimate=cost,
            name=name,
        )(*args)

    return run


def shape(dims, dtype):
    return jax.ShapeDtypeStruct(dims, dtype)


def slots_call(block, rows, m, labels, tokens, upstream):
    tok_rows, width = tokens.shape
    half_spec = pl.BlockSpec((tok_rows, width // 2), lambda i, m_ref: (0, m_ref[0]))
    return pl.pallas_call(
        functools.partial(slots_kernel, block),
        out_shape=pltpu.VMEM((rows, width // 2), BF16),
        grid_spec=pltpu.PrefetchScalarGridSpec(
            num_scalar_prefetch=1,
            grid=(1,),
            in_specs=[pl.BlockSpec(labels.shape, lambda i, m_ref: (0, 0)), half_spec, half_spec],
            out_specs=ONCHIP,
        ),
        compiler_params=PARAMS,
        name="slots",
    )(m, offchip(labels), offchip(tokens), offchip(upstream))


def front_call(block, mine, up_matrix, down_matrix):
    anywhere = pl.BlockSpec(memory_space=pl.ANY)
    return pl.pallas_call(
        functools.partial(front_kernel, block),
        out_shape=(
            pltpu.VMEM(mine.shape, BF16),
            pltpu.VMEM(up_matrix.shape, BF16),
            pltpu.VMEM(down_matrix.shape, BF16),
        ),
        in_specs=[ONCHIP, anywhere, anywhere],
        out_specs=(ONCHIP, ONCHIP, ONCHIP),
        scratch_shapes=[pltpu.SemaphoreType.DMA((2,))],
        compiler_params=PARAMS,
        name="front",
    )(onchip(mine), offchip(up_matrix), offchip(down_matrix))


def weight_grads(block, groups, m, group, mine, other, up_matrix, down_matrix):
    rows = mine.shape[0]
    width, hidden_cols = up_matrix.shape
    share = width // groups
    half = groups // 2
    vmem = pltpu.VMEM
    far_up, far_down, hidden, pre_grad, turned, hidden_t = pl.pallas_call(
        functools.partial(hidden_kernel, block, groups),
        out_shape=(
            vmem((hidden_cols, share), BF16),
            vmem((hidden_cols, share), BF16),
            vmem((rows // 2, hidden_cols), BF16),
            vmem((rows // 2, hidden_cols), BF16),
            vmem((rows, width), BF16),
            vmem((hidden_cols, rows // 2), BF16),
        ),
        in_specs=[pl.BlockSpec(memory_space=pltpu.SMEM)] * 2 + [ONCHIP] * 4,
        out_specs=(ONCHIP,) * 6,
        scratch_shapes=[vmem((rows, width), BF16)],
        compiler_params=PARAMS,
        name="hidden",
    )(m, group, onchip(mine), onchip(other), onchip(up_matrix), onchip(down_matrix))
    ahead = [(i, (i + 1) % groups) for i in range(groups)]
    behind = [(i, (i - 1) % groups) for i in range(groups)]
    right = lax.ppermute(far_up, "dp", ahead)
    left = lax.ppermute(far_down, "dp", behind)
    size = vmem((2 * hidden_cols, share), BF16)
    runs = ((0, half), (half + 1, groups))
    parts = call(functools.partial(shares_kernel, runs), (size,) * (groups - 1), 0, "shares")(
        onchip(turned), onchip(hidden_t), onchip(pre_grad)
    )
    parts = parts[:half] + (None,) + parts[half:]
    sent = []
    for hop in range(half - 1, 0, -1):
        whole = hop < half - 1
        step = call(functools.partial(hop_kernel, None if whole else False), size, 0, "ahead", 0, long(4) if hop == 1 else None)
        sent.append(step(onchip(right), onchip(parts[hop])))
        right = lax.ppermute(sent[-1], "dp", ahead)
        step = call(functools.partial(hop_kernel, None if whole else True), size, 0, "behind", 0, long(2) if hop == 1 else None)
        sent.append(step(onchip(left), onchip(parts[groups - hop])))
        left = lax.ppermute(sent[-1], "dp", behind)
    def finish(after):
        outs = (shape((share, hidden_cols), F32), shape((hidden_cols, share), F32))
        return call(last_kernel, outs, 0, "last", 1)(offchip(after), onchip(left), onchip(right), onchip(parts[0]))

    return finish, hidden, pre_grad, sent


def body(tokens, block_experts, weight_up, weight_down, upstream):
    experts = lax.axis_size("expert")
    groups = lax.axis_size("dp")
    blocks_dev = block_experts.shape[0]
    tok_rows, width = tokens.shape
    block = tok_rows // blocks_dev
    half_cols = width // 2
    rows = 2 * experts * block
    m = lax.axis_index("mp").astype(jnp.int32).reshape(1)
    labels = block_experts.reshape(1, blocks_dev)
    swap = [(0, 1), (1, 0)]

    def exchange(value):
        shaped = value.reshape(experts, 2 * block, half_cols)
        moved = lax.all_to_all(shaped, "expert", split_axis=0, concat_axis=0, tiled=True)
        return moved.reshape(rows, half_cols)

    slots = slots_call(block, rows, m, labels, tokens, upstream)
    arrived = exchange(slots)
    other = lax.ppermute(arrived, "mp", swap)
    mine, up_matrix, down_matrix = front_call(block, arrived, weight_up[0], weight_down[0])
    group = lax.axis_index("dp").astype(jnp.int32).reshape(1)
    finish, hidden, pre_grad, sent = weight_grads(block, groups, m, group, mine, other, up_matrix, down_matrix)

    keep, send = call(
        returns_kernel, (pltpu.VMEM((rows, half_cols), F32), pltpu.VMEM((rows, half_cols), BF16)), 1, "returns"
    )(m, onchip(hidden), onchip(pre_grad), onchip(up_matrix), onchip(down_matrix))
    got = lax.ppermute(send, "mp", swap)
    added = call(functools.partial(add_kernel, block), pltpu.VMEM((rows, half_cols), BF16), 0, "add", 2)(
        sent[2], sent[3], onchip(keep), onchip(got)
    )
    back = exchange(added)
    home = call(functools.partial(home_kernel, block), pltpu.VMEM((2 * tok_rows, half_cols), BF16), 0, "home")(
        labels, onchip(back)
    )
    home_other = lax.ppermute(home, "mp", swap)
    layer_output, grad_tokens = call(
        final_kernel, (shape(tokens.shape, F32), shape(tokens.shape, F32)), 1, "final"
    )(m, onchip(home), onchip(home_other), tokens, upstream)
    grad_up, grad_down = finish(grad_tokens)
    return (layer_output, grad_tokens, grad_up[None], grad_down[None])


def solution(mesh):
    placed = (
        P(("dp", "expert"), None),
        P(("dp", "expert"), None),
        P("expert", None, "mp"),
        P("expert", "mp", None),
        P(("dp", "expert"), None),
    )
    return jax.shard_map(
        body,
        mesh=mesh,
        in_specs=placed,
        out_specs=(
            P(("dp", "expert"), None),
            P(("dp", "expert"), None),
            P("expert", "dp", "mp"),
            P("expert", "mp", "dp"),
        ),
        check_vma=False,
    )
```

```python
import functools

import jax
import jax.numpy as jnp
from jax import lax
from jax.experimental import pallas as pl
from jax.experimental.pallas import tpu as pltpu
from jax.sharding import PartitionSpec as P

F32 = jnp.float32
BF16 = jnp.bfloat16
GELU_C = 0.7978845608028654
GELU_A = 0.044715
NN = (((1,), (0,)), ((), ()))
NT = (((1,), (1,)), ((), ()))
TN = (((0,), (0,)), ((), ()))


def iota(shape, axis):
    return lax.broadcasted_iota(jnp.int32, shape, axis)


def mm(a, b, dims):
    return lax.dot_general(a, b, dims, preferred_element_type=F32)


def label_column(labels):
    blocks = labels.shape[1]
    eye = iota((blocks, blocks), 0) == iota((blocks, blocks), 1)
    return jnp.sum(jnp.where(eye, labels, 0), axis=1, keepdims=True)


def slots_kernel(block, m_ref, labels_ref, tok_ref, up_ref, out_ref):
    rows = tok_ref.shape[0]
    blocks = labels_ref.shape[1]
    column = label_column(labels_ref[...])
    spread = iota((blocks, rows), 1) // block == iota((blocks, rows), 0)
    label_row = jnp.sum(jnp.where(spread, column, 0), axis=0, keepdims=True)
    dest = label_row * (2 * block) + iota((1, rows), 1) % block
    out_rows = iota((out_ref.shape[0], rows), 0)
    pick_tok = (out_rows == dest).astype(F32).astype(BF16)
    pick_up = (out_rows == dest + block).astype(F32).astype(BF16)
    total = mm(pick_tok, tok_ref[...].astype(BF16), NN)
    total = total + mm(pick_up, up_ref[...].astype(BF16), NN)
    out_ref[...] = total.astype(BF16)


def split_rows(rows, block):
    half = rows // 2
    i = iota((rows, rows), 0)
    j = lax.rem(i, half)
    source = (j // block) * (2 * block) + lax.rem(j, block) + jnp.where(i >= half, block, 0)
    return (iota((rows, rows), 1) == source).astype(F32).astype(BF16)


def merge_rows(rows, block):
    half = rows // 2
    i = iota((rows, rows), 1)
    j = lax.rem(i, half)
    source = (j // block) * (2 * block) + lax.rem(j, block) + jnp.where(i >= half, block, 0)
    return (iota((rows, rows), 0) == source).astype(F32).astype(BF16)


def front_kernel(block, mine_ref, up_ref, down_ref, x_ref, up_out, down_out, sems):
    copies = [
        pltpu.make_async_copy(up_ref, up_out, sems.at[0]),
        pltpu.make_async_copy(down_ref, down_out, sems.at[1]),
    ]
    for copy in copies:
        copy.start()
    x_ref[...] = mm(split_rows(mine_ref.shape[0], block), mine_ref[...], NN).astype(BF16)
    for copy in copies:
        copy.wait()


def hidden_kernel(
    block, groups, m_ref, group_ref, mine_ref, other_ref, up_ref, down_ref,
    far_up_ref, far_down_ref, hid_ref, pg_ref, turned_ref, hidt_ref, x_ref,
):
    rows, half_cols = mine_ref.shape
    half = rows // 2
    share = turned_ref.shape[1] // groups
    first = m_ref[0] == 0
    mine = mine_ref[...]
    other = mm(split_rows(rows, block), other_ref[...], NN).astype(BF16)
    x_ref[:, :half_cols] = jnp.where(first, mine, other)
    x_ref[:, half_cols:] = jnp.where(first, other, mine)
    for k in range(groups):
        owner = lax.rem(group_ref[0] + k, groups)
        turned_ref[:, k * share : (k + 1) * share] = x_ref[:, pl.ds(pl.multiple_of(owner * share, share), share)]
    pre = mm(x_ref[:half, :], up_ref[...], NN)
    hidden_grad = mm(x_ref[half:, :], down_ref[...], NT)
    square = pre * pre
    t = jnp.tanh(GELU_C * (pre + GELU_A * (square * pre)))
    cdf = 0.5 * (1.0 + t)
    slope = cdf + 0.5 * pre * (1.0 - t * t) * (GELU_C * (1.0 + 3.0 * GELU_A * square))
    hidden = (pre * cdf).astype(BF16)
    hid_ref[...] = hidden
    hidt_ref[...] = hidden.T
    pg_ref[...] = (hidden_grad * slope).astype(BF16)
    far = slice(groups // 2 * share, (groups // 2 + 1) * share)
    up_share(far_up_ref, 0, mm(turned_ref[:half, far], pg_ref[...], TN).astype(BF16))
    far_down_ref[...] = mm(hidt_ref[...], turned_ref[half:, far], NN).astype(BF16)


def up_share(ref, base, value):
    share = value.shape[0]
    for j in range(value.shape[1] // share):
        ref[base + j * share : base + (j + 1) * share, :] = value[:, j * share : (j + 1) * share]


def shares_kernel(slots, turned_ref, hidt_ref, pg_ref, *part_refs):
    half = pg_ref.shape[0]
    hidden_cols, share = hidt_ref.shape[0], part_refs[0].shape[1]
    done = 0
    for first, last in slots:
        cols = slice(first * share, last * share)
        up_part = mm(turned_ref[:half, cols], pg_ref[...], TN).astype(BF16)
        down_part = mm(hidt_ref[...], turned_ref[half:, cols], NN).astype(BF16)
        for k in range(last - first):
            own = slice(k * share, (k + 1) * share)
            up_share(part_refs[done], 0, up_part[own, :])
            part_refs[done][hidden_cols:, :] = down_part[:, own]
            done += 1


def hop_kernel(lower, got_ref, part_ref, out_ref):
    half = out_ref.shape[0] // 2
    if lower is None:
        out_ref[...] = (part_ref[...].astype(F32) + got_ref[...].astype(F32)).astype(BF16)
        return
    came = slice(half, 2 * half) if lower else slice(0, half)
    fresh = slice(0, half) if lower else slice(half, 2 * half)
    out_ref[came, :] = (part_ref[came, :].astype(F32) + got_ref[...].astype(F32)).astype(BF16)
    out_ref[fresh, :] = part_ref[fresh, :]


def last_kernel(after_ref, left_ref, right_ref, part_ref, up_ref, down_ref):
    del after_ref
    hidden_cols, share = down_ref.shape

    def total(at):
        return part_ref[at, :].astype(F32) + (left_ref[at, :].astype(F32) + right_ref[at, :].astype(F32))

    for j in range(hidden_cols // share):
        at = slice(j * share, (j + 1) * share)
        up_ref[:, at] = total(at)
    down_ref[...] = total(slice(hidden_cols, 2 * hidden_cols))


def returns_kernel(m_ref, hid_ref, pg_ref, up_ref, down_ref, keep_ref, send_ref):
    half = hid_ref.shape[0]
    half_cols = keep_ref.shape[1]
    first = m_ref[0] == 0
    mixed = mm(hid_ref[...], down_ref[...], NN)
    tgrad = mm(pg_ref[...], up_ref[...], NT)
    for k, value in ((0, mixed), (1, tgrad)):
        low, high = value[:, :half_cols], value[:, half_cols:]
        at = slice(k * half, (k + 1) * half)
        keep_ref[at, :] = jnp.where(first, low, high)
        send_ref[at, :] = jnp.where(first, high, low).astype(BF16)


def add_kernel(block, after_ref, also_ref, keep_ref, got_ref, out_ref):
    del after_ref, also_ref
    total = (keep_ref[...] + got_ref[...].astype(F32)).astype(BF16)
    out_ref[...] = mm(merge_rows(total.shape[0], block), total, NN).astype(BF16)


def home_kernel(block, labels_ref, back_ref, out_ref):
    rows = out_ref.shape[0] // 2
    blocks = labels_ref.shape[1]
    spread = iota((rows, blocks), 0) // block == iota((rows, blocks), 1)
    label = jnp.sum(jnp.where(spread, labels_ref[...], 0), axis=1, keepdims=True)
    dest = label * (2 * block) + iota((rows, 1), 0) % block
    columns = iota((rows, back_ref.shape[0]), 1)
    back = back_ref[...]
    for k in range(2):
        pick = (columns == dest + k * block).astype(F32).astype(BF16)
        out_ref[k * rows : (k + 1) * rows, :] = mm(pick, back, NN).astype(BF16)


def final_kernel(m_ref, mine_ref, other_ref, tok_ref, up_ref, out_ref, grad_ref):
    rows = tok_ref.shape[0]
    half_cols = mine_ref.shape[1]
    first = m_ref[0] == 0
    mine = mine_ref[...].astype(F32)
    other = other_ref[...].astype(F32)
    low = jnp.where(first, mine, other)
    high = jnp.where(first, other, mine)
    out_ref[:, :half_cols] = tok_ref[:, :half_cols] + low[:rows]
    out_ref[:, half_cols:] = tok_ref[:, half_cols:] + high[:rows]
    grad_ref[:, :half_cols] = up_ref[:, :half_cols] + low[rows:]
    grad_ref[:, half_cols:] = up_ref[:, half_cols:] + high[rows:]


PARAMS = pltpu.CompilerParams(vmem_limit_bytes=16 * 2**20)
ONCHIP = pl.BlockSpec(memory_space=pltpu.VMEM)


def onchip(array):
    return pltpu.with_memory_space_constraint(array, pltpu.VMEM)


def offchip(array):
    return pltpu.with_memory_space_constraint(array, pltpu.HBM)


def call(kernel, outs, scalars, name, after=0):
    one = not isinstance(outs, tuple)
    unread = [pl.BlockSpec(memory_space=pl.ANY)] * after

    def run(*args):
        arrays = len(args) - scalars - after
        return pl.pallas_call(
            kernel,
            out_shape=outs,
            in_specs=[pl.BlockSpec(memory_space=pltpu.SMEM)] * scalars + unread + [ONCHIP] * arrays,
            out_specs=ONCHIP if one else (ONCHIP,) * len(outs),
            compiler_params=PARAMS,
            name=name,
        )(*args)

    return run


def shape(dims, dtype):
    return jax.ShapeDtypeStruct(dims, dtype)


def slots_call(block, rows, m, labels, tokens, upstream):
    tok_rows, width = tokens.shape
    half_spec = pl.BlockSpec((tok_rows, width // 2), lambda i, m_ref: (0, m_ref[0]))
    return pl.pallas_call(
        functools.partial(slots_kernel, block),
        out_shape=pltpu.VMEM((rows, width // 2), BF16),
        grid_spec=pltpu.PrefetchScalarGridSpec(
            num_scalar_prefetch=1,
            grid=(1,),
            in_specs=[pl.BlockSpec(labels.shape, lambda i, m_ref: (0, 0)), half_spec, half_spec],
            out_specs=ONCHIP,
        ),
        compiler_params=PARAMS,
        name="slots",
    )(m, offchip(labels), offchip(tokens), offchip(upstream))


def front_call(block, mine, up_matrix, down_matrix):
    anywhere = pl.BlockSpec(memory_space=pl.ANY)
    return pl.pallas_call(
        functools.partial(front_kernel, block),
        out_shape=(
            pltpu.VMEM(mine.shape, BF16),
            pltpu.VMEM(up_matrix.shape, BF16),
            pltpu.VMEM(down_matrix.shape, BF16),
        ),
        in_specs=[ONCHIP, anywhere, anywhere],
        out_specs=(ONCHIP, ONCHIP, ONCHIP),
        scratch_shapes=[pltpu.SemaphoreType.DMA((2,))],
        compiler_params=PARAMS,
        name="front",
    )(onchip(mine), offchip(up_matrix), offchip(down_matrix))


def weight_grads(block, groups, m, group, mine, other, up_matrix, down_matrix):
    rows = mine.shape[0]
    width, hidden_cols = up_matrix.shape
    share = width // groups
    half = groups // 2
    vmem = pltpu.VMEM
    far_up, far_down, hidden, pre_grad, turned, hidden_t = pl.pallas_call(
        functools.partial(hidden_kernel, block, groups),
        out_shape=(
            vmem((hidden_cols, share), BF16),
            vmem((hidden_cols, share), BF16),
            vmem((rows // 2, hidden_cols), BF16),
            vmem((rows // 2, hidden_cols), BF16),
            vmem((rows, width), BF16),
            vmem((hidden_cols, rows // 2), BF16),
        ),
        in_specs=[pl.BlockSpec(memory_space=pltpu.SMEM)] * 2 + [ONCHIP] * 4,
        out_specs=(ONCHIP,) * 6,
        scratch_shapes=[vmem((rows, width), BF16)],
        compiler_params=PARAMS,
        name="hidden",
    )(m, group, onchip(mine), onchip(other), onchip(up_matrix), onchip(down_matrix))
    ahead = [(i, (i + 1) % groups) for i in range(groups)]
    behind = [(i, (i - 1) % groups) for i in range(groups)]
    right = lax.ppermute(far_up, "dp", ahead)
    left = lax.ppermute(far_down, "dp", behind)
    size = vmem((2 * hidden_cols, share), BF16)
    runs = ((0, half), (half + 1, groups))
    parts = call(functools.partial(shares_kernel, runs), (size,) * (groups - 1), 0, "shares")(
        onchip(turned), onchip(hidden_t), onchip(pre_grad)
    )
    parts = parts[:half] + (None,) + parts[half:]
    sent = []
    for hop in range(half - 1, 0, -1):
        whole = hop < half - 1
        step = call(functools.partial(hop_kernel, None if whole else False), size, 0, "ahead")
        sent.append(step(onchip(right), onchip(parts[hop])))
        right = lax.ppermute(sent[-1], "dp", ahead)
        step = call(functools.partial(hop_kernel, None if whole else True), size, 0, "behind")
        sent.append(step(onchip(left), onchip(parts[groups - hop])))
        left = lax.ppermute(sent[-1], "dp", behind)
    def finish(after):
        outs = (shape((share, hidden_cols), F32), shape((hidden_cols, share), F32))
        return call(last_kernel, outs, 0, "last", 1)(offchip(after), onchip(left), onchip(right), offchip(parts[0]))

    return finish, hidden, pre_grad, sent


def body(tokens, block_experts, weight_up, weight_down, upstream):
    experts = lax.axis_size("expert")
    groups = lax.axis_size("dp")
    blocks_dev = block_experts.shape[0]
    tok_rows, width = tokens.shape
    block = tok_rows // blocks_dev
    half_cols = width // 2
    rows = 2 * experts * block
    m = lax.axis_index("mp").astype(jnp.int32).reshape(1)
    labels = block_experts.reshape(1, blocks_dev)
    swap = [(0, 1), (1, 0)]

    def exchange(value):
        shaped = value.reshape(experts, 2 * block, half_cols)
        moved = lax.all_to_all(shaped, "expert", split_axis=0, concat_axis=0, tiled=True)
        return moved.reshape(rows, half_cols)

    slots = slots_call(block, rows, m, labels, tokens, upstream)
    arrived = exchange(slots)
    other = lax.ppermute(arrived, "mp", swap)
    mine, up_matrix, down_matrix = front_call(block, arrived, weight_up[0], weight_down[0])
    group = lax.axis_index("dp").astype(jnp.int32).reshape(1)
    finish, hidden, pre_grad, sent = weight_grads(block, groups, m, group, mine, other, up_matrix, down_matrix)

    keep, send = call(
        returns_kernel, (pltpu.VMEM((rows, half_cols), F32), pltpu.VMEM((rows, half_cols), BF16)), 1, "returns"
    )(m, onchip(hidden), onchip(pre_grad), onchip(up_matrix), onchip(down_matrix))
    got = lax.ppermute(send, "mp", swap)
    added = call(functools.partial(add_kernel, block), pltpu.VMEM((rows, half_cols), BF16), 0, "add", 2)(
        sent[0], sent[1], onchip(keep), onchip(got)
    )
    back = exchange(added)
    home = call(functools.partial(home_kernel, block), pltpu.VMEM((2 * tok_rows, half_cols), BF16), 0, "home")(
        labels, onchip(back)
    )
    home_other = lax.ppermute(home, "mp", swap)
    layer_output, grad_tokens = call(
        final_kernel, (shape(tokens.shape, F32), shape(tokens.shape, F32)), 1, "final"
    )(m, onchip(home), onchip(home_other), tokens, upstream)
    grad_up, grad_down = finish(grad_tokens)
    return (layer_output, grad_tokens, grad_up[None], grad_down[None])


def solution(mesh):
    placed = (
        P(("dp", "expert"), None),
        P(("dp", "expert"), None),
        P("expert", None, "mp"),
        P("expert", "mp", None),
        P(("dp", "expert"), None),
    )
    return jax.shard_map(
        body,
        mesh=mesh,
        in_specs=placed,
        out_specs=(
            P(("dp", "expert"), None),
            P(("dp", "expert"), None),
            P("expert", "dp", "mp"),
            P("expert", "mp", "dp"),
        ),
        check_vma=False,
    )
```

```python
import functools

import jax
import jax.numpy as jnp
from jax import lax
from jax.experimental import pallas as pl
from jax.experimental.pallas import tpu as pltpu
from jax.sharding import PartitionSpec as P

F32 = jnp.float32
BF16 = jnp.bfloat16
GELU_C = 0.7978845608028654
GELU_A = 0.044715
NN = (((1,), (0,)), ((), ()))
NT = (((1,), (1,)), ((), ()))
TN = (((0,), (0,)), ((), ()))


def iota(shape, axis):
    return lax.broadcasted_iota(jnp.int32, shape, axis)


def mm(a, b, dims):
    return lax.dot_general(a, b, dims, preferred_element_type=F32)


def label_column(labels):
    blocks = labels.shape[1]
    eye = iota((blocks, blocks), 0) == iota((blocks, blocks), 1)
    return jnp.sum(jnp.where(eye, labels, 0), axis=1, keepdims=True)


def slots_kernel(block, m_ref, labels_ref, tok_ref, up_ref, out_ref):
    rows = tok_ref.shape[0]
    blocks = labels_ref.shape[1]
    column = label_column(labels_ref[...])
    spread = iota((blocks, rows), 1) // block == iota((blocks, rows), 0)
    label_row = jnp.sum(jnp.where(spread, column, 0), axis=0, keepdims=True)
    dest = label_row * (2 * block) + iota((1, rows), 1) % block
    out_rows = iota((out_ref.shape[0], rows), 0)
    pick_tok = (out_rows == dest).astype(F32).astype(BF16)
    pick_up = (out_rows == dest + block).astype(F32).astype(BF16)
    total = mm(pick_tok, tok_ref[...].astype(BF16), NN)
    total = total + mm(pick_up, up_ref[...].astype(BF16), NN)
    out_ref[...] = total.astype(BF16)


def split_rows(rows, block):
    half = rows // 2
    i = iota((rows, rows), 0)
    j = lax.rem(i, half)
    source = (j // block) * (2 * block) + lax.rem(j, block) + jnp.where(i >= half, block, 0)
    return (iota((rows, rows), 1) == source).astype(F32).astype(BF16)


def merge_rows(rows, block):
    half = rows // 2
    i = iota((rows, rows), 1)
    j = lax.rem(i, half)
    source = (j // block) * (2 * block) + lax.rem(j, block) + jnp.where(i >= half, block, 0)
    return (iota((rows, rows), 0) == source).astype(F32).astype(BF16)


def front_kernel(block, mine_ref, up_ref, down_ref, x_ref, up_out, down_out, sems):
    copies = [
        pltpu.make_async_copy(up_ref, up_out, sems.at[0]),
        pltpu.make_async_copy(down_ref, down_out, sems.at[1]),
    ]
    for copy in copies:
        copy.start()
    x_ref[...] = mm(split_rows(mine_ref.shape[0], block), mine_ref[...], NN).astype(BF16)
    for copy in copies:
        copy.wait()


def hidden_kernel(
    block, groups, m_ref, group_ref, mine_ref, other_ref, up_ref, down_ref,
    far_up_ref, far_down_ref, hid_ref, pg_ref, turned_ref, hidt_ref, x_ref,
):
    rows, half_cols = mine_ref.shape
    half = rows // 2
    share = turned_ref.shape[1] // groups
    first = m_ref[0] == 0
    mine = mine_ref[...]
    other = mm(split_rows(rows, block), other_ref[...], NN).astype(BF16)
    x_ref[:, :half_cols] = jnp.where(first, mine, other)
    x_ref[:, half_cols:] = jnp.where(first, other, mine)
    for k in range(groups):
        owner = lax.rem(group_ref[0] + k, groups)
        turned_ref[:, k * share : (k + 1) * share] = x_ref[:, pl.ds(pl.multiple_of(owner * share, share), share)]
    pre = mm(x_ref[:half, :], up_ref[...], NN)
    hidden_grad = mm(x_ref[half:, :], down_ref[...], NT)
    square = pre * pre
    t = jnp.tanh(GELU_C * (pre + GELU_A * (square * pre)))
    cdf = 0.5 * (1.0 + t)
    slope = cdf + 0.5 * pre * (1.0 - t * t) * (GELU_C * (1.0 + 3.0 * GELU_A * square))
    hidden = (pre * cdf).astype(BF16)
    hid_ref[...] = hidden
    hidt_ref[...] = hidden.T
    pg_ref[...] = (hidden_grad * slope).astype(BF16)
    far = slice(groups // 2 * share, (groups // 2 + 1) * share)
    up_share(far_up_ref, 0, mm(turned_ref[:half, far], pg_ref[...], TN).astype(BF16))
    far_down_ref[...] = mm(hidt_ref[...], turned_ref[half:, far], NN).astype(BF16)


def up_share(ref, base, value):
    share = value.shape[0]
    for j in range(value.shape[1] // share):
        ref[base + j * share : base + (j + 1) * share, :] = value[:, j * share : (j + 1) * share]


def shares_kernel(slots, turned_ref, hidt_ref, pg_ref, *part_refs):
    half = pg_ref.shape[0]
    hidden_cols, share = hidt_ref.shape[0], part_refs[0].shape[1]
    done = 0
    for first, last in slots:
        cols = slice(first * share, last * share)
        up_part = mm(turned_ref[:half, cols], pg_ref[...], TN).astype(BF16)
        down_part = mm(hidt_ref[...], turned_ref[half:, cols], NN).astype(BF16)
        for k in range(last - first):
            own = slice(k * share, (k + 1) * share)
            up_share(part_refs[done], 0, up_part[own, :])
            part_refs[done][hidden_cols:, :] = down_part[:, own]
            done += 1


def hop_kernel(lower, got_ref, part_ref, out_ref):
    half = out_ref.shape[0] // 2
    if lower is None:
        out_ref[...] = (part_ref[...].astype(F32) + got_ref[...].astype(F32)).astype(BF16)
        return
    came = slice(half, 2 * half) if lower else slice(0, half)
    fresh = slice(0, half) if lower else slice(half, 2 * half)
    out_ref[came, :] = (part_ref[came, :].astype(F32) + got_ref[...].astype(F32)).astype(BF16)
    out_ref[fresh, :] = part_ref[fresh, :]


def last_kernel(after_ref, left_ref, right_ref, part_ref, up_ref, down_ref):
    del after_ref
    hidden_cols, share = down_ref.shape

    def total(at):
        return part_ref[at, :].astype(F32) + (left_ref[at, :].astype(F32) + right_ref[at, :].astype(F32))

    for j in range(hidden_cols // share):
        at = slice(j * share, (j + 1) * share)
        up_ref[:, at] = total(at)
    down_ref[...] = total(slice(hidden_cols, 2 * hidden_cols))


def returns_kernel(m_ref, hid_ref, pg_ref, up_ref, down_ref, keep_ref, send_ref):
    half = hid_ref.shape[0]
    half_cols = keep_ref.shape[1]
    first = m_ref[0] == 0
    mixed = mm(hid_ref[...], down_ref[...], NN)
    tgrad = mm(pg_ref[...], up_ref[...], NT)
    for k, value in ((0, mixed), (1, tgrad)):
        low, high = value[:, :half_cols], value[:, half_cols:]
        at = slice(k * half, (k + 1) * half)
        keep_ref[at, :] = jnp.where(first, low, high)
        send_ref[at, :] = jnp.where(first, high, low).astype(BF16)


def add_kernel(block, after_ref, also_ref, keep_ref, got_ref, out_ref):
    del after_ref, also_ref
    total = (keep_ref[...] + got_ref[...].astype(F32)).astype(BF16)
    out_ref[...] = mm(merge_rows(total.shape[0], block), total, NN).astype(BF16)


def home_kernel(block, labels_ref, back_ref, out_ref):
    rows = out_ref.shape[0] // 2
    blocks = labels_ref.shape[1]
    spread = iota((rows, blocks), 0) // block == iota((rows, blocks), 1)
    label = jnp.sum(jnp.where(spread, labels_ref[...], 0), axis=1, keepdims=True)
    dest = label * (2 * block) + iota((rows, 1), 0) % block
    columns = iota((rows, back_ref.shape[0]), 1)
    back = back_ref[...]
    for k in range(2):
        pick = (columns == dest + k * block).astype(F32).astype(BF16)
        out_ref[k * rows : (k + 1) * rows, :] = mm(pick, back, NN).astype(BF16)


def final_kernel(m_ref, mine_ref, other_ref, tok_ref, up_ref, out_ref, grad_ref):
    rows = tok_ref.shape[0]
    half_cols = mine_ref.shape[1]
    first = m_ref[0] == 0
    mine = mine_ref[...].astype(F32)
    other = other_ref[...].astype(F32)
    low = jnp.where(first, mine, other)
    high = jnp.where(first, other, mine)
    out_ref[:, :half_cols] = tok_ref[:, :half_cols] + low[:rows]
    out_ref[:, half_cols:] = tok_ref[:, half_cols:] + high[:rows]
    grad_ref[:, :half_cols] = up_ref[:, :half_cols] + low[rows:]
    grad_ref[:, half_cols:] = up_ref[:, half_cols:] + high[rows:]


PARAMS = pltpu.CompilerParams(vmem_limit_bytes=16 * 2**20)
ONCHIP = pl.BlockSpec(memory_space=pltpu.VMEM)


def onchip(array):
    return pltpu.with_memory_space_constraint(array, pltpu.VMEM)


def offchip(array):
    return pltpu.with_memory_space_constraint(array, pltpu.HBM)


def call(kernel, outs, scalars, name, after=0):
    one = not isinstance(outs, tuple)
    unread = [pl.BlockSpec(memory_space=pl.ANY)] * after

    def run(*args):
        arrays = len(args) - scalars - after
        return pl.pallas_call(
            kernel,
            out_shape=outs,
            in_specs=[pl.BlockSpec(memory_space=pltpu.SMEM)] * scalars + unread + [ONCHIP] * arrays,
            out_specs=ONCHIP if one else (ONCHIP,) * len(outs),
            compiler_params=PARAMS,
            name=name,
        )(*args)

    return run


def shape(dims, dtype):
    return jax.ShapeDtypeStruct(dims, dtype)


def slots_call(block, rows, m, labels, tokens, upstream):
    tok_rows, width = tokens.shape
    half_spec = pl.BlockSpec((tok_rows, width // 2), lambda i, m_ref: (0, m_ref[0]))
    return pl.pallas_call(
        functools.partial(slots_kernel, block),
        out_shape=pltpu.VMEM((rows, width // 2), BF16),
        grid_spec=pltpu.PrefetchScalarGridSpec(
            num_scalar_prefetch=1,
            grid=(1,),
            in_specs=[pl.BlockSpec(labels.shape, lambda i, m_ref: (0, 0)), half_spec, half_spec],
            out_specs=ONCHIP,
        ),
        compiler_params=PARAMS,
        name="slots",
    )(m, offchip(labels), offchip(tokens), offchip(upstream))


def front_call(block, mine, up_matrix, down_matrix):
    anywhere = pl.BlockSpec(memory_space=pl.ANY)
    return pl.pallas_call(
        functools.partial(front_kernel, block),
        out_shape=(
            pltpu.VMEM(mine.shape, BF16),
            pltpu.VMEM(up_matrix.shape, BF16),
            pltpu.VMEM(down_matrix.shape, BF16),
        ),
        in_specs=[ONCHIP, anywhere, anywhere],
        out_specs=(ONCHIP, ONCHIP, ONCHIP),
        scratch_shapes=[pltpu.SemaphoreType.DMA((2,))],
        compiler_params=PARAMS,
        name="front",
    )(onchip(mine), offchip(up_matrix), offchip(down_matrix))


def weight_grads(block, groups, m, group, mine, other, up_matrix, down_matrix):
    rows = mine.shape[0]
    width, hidden_cols = up_matrix.shape
    share = width // groups
    half = groups // 2
    vmem = pltpu.VMEM
    far_up, far_down, hidden, pre_grad, turned, hidden_t = pl.pallas_call(
        functools.partial(hidden_kernel, block, groups),
        out_shape=(
            vmem((hidden_cols, share), BF16),
            vmem((hidden_cols, share), BF16),
            vmem((rows // 2, hidden_cols), BF16),
            vmem((rows // 2, hidden_cols), BF16),
            vmem((rows, width), BF16),
            vmem((hidden_cols, rows // 2), BF16),
        ),
        in_specs=[pl.BlockSpec(memory_space=pltpu.SMEM)] * 2 + [ONCHIP] * 4,
        out_specs=(ONCHIP,) * 6,
        scratch_shapes=[vmem((rows, width), BF16)],
        compiler_params=PARAMS,
        name="hidden",
    )(m, group, onchip(mine), onchip(other), onchip(up_matrix), onchip(down_matrix))
    ahead = [(i, (i + 1) % groups) for i in range(groups)]
    behind = [(i, (i - 1) % groups) for i in range(groups)]
    right = lax.ppermute(far_up, "dp", ahead)
    left = lax.ppermute(far_down, "dp", behind)
    size = vmem((2 * hidden_cols, share), BF16)
    runs = ((0, half), (half + 1, groups))
    parts = call(functools.partial(shares_kernel, runs), (size,) * (groups - 1), 0, "shares")(
        onchip(turned), onchip(hidden_t), onchip(pre_grad)
    )
    parts = parts[:half] + (None,) + parts[half:]
    sent = []
    for hop in range(half - 1, 0, -1):
        whole = hop < half - 1
        step = call(functools.partial(hop_kernel, None if whole else False), size, 0, "ahead")
        sent.append(step(onchip(right), onchip(parts[hop])))
        right = lax.ppermute(sent[-1], "dp", ahead)
        step = call(functools.partial(hop_kernel, None if whole else True), size, 0, "behind")
        sent.append(step(onchip(left), onchip(parts[groups - hop])))
        left = lax.ppermute(sent[-1], "dp", behind)
    def finish(after):
        outs = (shape((share, hidden_cols), F32), shape((hidden_cols, share), F32))
        return call(last_kernel, outs, 0, "last", 1)(offchip(after), onchip(left), onchip(right), offchip(parts[0]))

    return finish, hidden, pre_grad, sent


def body(tokens, block_experts, weight_up, weight_down, upstream):
    experts = lax.axis_size("expert")
    groups = lax.axis_size("dp")
    blocks_dev = block_experts.shape[0]
    tok_rows, width = tokens.shape
    block = tok_rows // blocks_dev
    half_cols = width // 2
    rows = 2 * experts * block
    m = lax.axis_index("mp").astype(jnp.int32).reshape(1)
    labels = block_experts.reshape(1, blocks_dev)
    swap = [(0, 1), (1, 0)]

    def exchange(value):
        shaped = value.reshape(experts, 2 * block, half_cols)
        moved = lax.all_to_all(shaped, "expert", split_axis=0, concat_axis=0, tiled=True)
        return moved.reshape(rows, half_cols)

    slots = slots_call(block, rows, m, labels, tokens, upstream)
    arrived = exchange(slots)
    other = lax.ppermute(arrived, "mp", swap)
    mine, up_matrix, down_matrix = front_call(block, arrived, weight_up[0], weight_down[0])
    group = lax.axis_index("dp").astype(jnp.int32).reshape(1)
    finish, hidden, pre_grad, sent = weight_grads(block, groups, m, group, mine, other, up_matrix, down_matrix)

    keep, send = call(
        returns_kernel, (pltpu.VMEM((rows, half_cols), F32), pltpu.VMEM((rows, half_cols), BF16)), 1, "returns"
    )(m, onchip(hidden), onchip(pre_grad), onchip(up_matrix), onchip(down_matrix))
    got = lax.ppermute(send, "mp", swap)
    added = call(functools.partial(add_kernel, block), pltpu.VMEM((rows, half_cols), BF16), 0, "add", 2)(
        sent[1], sent[0], onchip(keep), onchip(got)
    )
    back = exchange(added)
    home = call(functools.partial(home_kernel, block), pltpu.VMEM((2 * tok_rows, half_cols), BF16), 0, "home")(
        labels, onchip(back)
    )
    home_other = lax.ppermute(home, "mp", swap)
    layer_output, grad_tokens = call(
        final_kernel, (shape(tokens.shape, F32), shape(tokens.shape, F32)), 1, "final"
    )(m, onchip(home), onchip(home_other), tokens, upstream)
    grad_up, grad_down = finish(grad_tokens)
    return (layer_output, grad_tokens, grad_up[None], grad_down[None])


def solution(mesh):
    placed = (
        P(("dp", "expert"), None),
        P(("dp", "expert"), None),
        P("expert", None, "mp"),
        P("expert", "mp", None),
        P(("dp", "expert"), None),
    )
    return jax.shard_map(
        body,
        mesh=mesh,
        in_specs=placed,
        out_specs=(
            P(("dp", "expert"), None),
            P(("dp", "expert"), None),
            P("expert", "dp", "mp"),
            P("expert", "mp", "dp"),
        ),
        check_vma=False,
    )
```
